32 devices in a mesh: freq: 32 (over z, y, x, core).
Axes of the slice: x: 2, y: 2, z: 4, core: 2. Of those that a mesh axis runs over, the one named last changes fastest.
Arguments:
- model_vis: bfloat16 [64, 8, 4096], P('freq'), may hold values from -6 to 6
- observed: float32 [64, 4096], P('freq'), may hold values from -48 to 48
- row_keep: int32 [64, 4096], P('freq'), may hold values 0 or 1
- station_one: int32 [4096], replicated, may hold values from 0 to 61, as said below
- station_two: int32 [4096], replicated, may hold values from 0 to 61
- smoothness: float32 [496], replicated, may hold values from 4 to 24576
Outputs:
- gains: float32 [64, 496], P('freq')
The draws below stay inside these ranges and needn't reach their ends.
Inputs may be any that keep to these rules, and one draw needn't show every extreme that they name: station_one and station_two differ in every row.
All inputs are finite; a program needn't handle non-finite values. No bound on the sum of `row_keep` on one device may be relied on, other than what follows from the above.
Results may differ from the reference program's by a relative error of at most 0.0003.
Values sent between devices are 32-bit elements; how exact they have to be, the bound alone decides.
A program may use at most 256 MiB of HBM per device.

```python
import math
import jax
import jax.numpy as jnp
from jax import lax

STATIONS = 62
DIRECTIONS = 8
ROWS = 4096
BLOCK = 496
CHANNELS = 64


def station_pairs(key):
    folded = jax.random.fold_in(key, 31)
    first_key, offset_key = jax.random.split(folded)
    leading = jax.random.randint(first_key, (ROWS,), 0, STATIONS, dtype=jnp.int32)
    offset = jax.random.randint(offset_key, (ROWS,), 1, STATIONS, dtype=jnp.int32)
    return (leading, (leading + offset) % STATIONS)


def draw_station_one(key, part):
    return station_pairs(key)[0]


def draw_station_two(key, part):
    return station_pairs(key)[1]


def draw_model_vis(key, part):
    folded = jax.random.fold_in(key, 53)
    value_key, pick_key = jax.random.split(folded)
    values = jax.random.truncated_normal(value_key, -6.0, 6.0, (CHANNELS, DIRECTIONS, ROWS), jnp.float32)
    faint_direction = jax.random.randint(pick_key, (), 0, DIRECTIONS, dtype=jnp.int32)
    channel_index = jnp.arange(CHANNELS, dtype=jnp.int32)
    direction_index = jnp.arange(DIRECTIONS, dtype=jnp.int32)
    faint = (channel_index[:, None] < CHANNELS // 2) & (direction_index[None, :] == faint_direction)
    factor = jnp.where(faint, 0.01, 1.0).astype(jnp.float32)
    return (values * factor[:, :, None]).astype(jnp.bfloat16)


def with_ends(array, own_key, smallest, top_value):
    shape = array.shape
    index_at = [jax.random.randint(jax.random.fold_in(own_key, axis), (), 0, shape[axis]) for axis in range(len(shape))]
    array = array.at[tuple(index_at)].set(smallest)
    longest = shape.index(max(shape))
    index_at[longest] = (index_at[longest] + 1) % shape[longest]
    return array.at[tuple(index_at)].set(top_value)


def block_levels(own_key, dims, cuts, low, largest):
    loudness = 1.0
    for dim, blocks in cuts:
        heights = jax.random.uniform(jax.random.fold_in(jax.random.fold_in(own_key, 6), dim), (blocks,), jnp.float32, low / len(cuts), largest / len(cuts))
        loudness = loudness * jnp.repeat(jnp.exp(heights), dims[dim] // blocks).reshape((-1,) + (1,) * (len(dims) - 1 - dim))
    return loudness


def centred(stream_key, dims, scale, limit, shards=(), held_as=jnp.bfloat16):
    array = scale * jax.random.normal(stream_key, dims, jnp.float32)
    if shards:
        array = array * block_levels(stream_key, dims, shards, -0.22, 0.18)
    return jnp.clip(array, -limit, limit).astype(held_as)


def setup_inputs(seed: int = 0) -> dict:
    seeds = jax.random.split(jax.random.key(seed), 7)
    return {
        "model_vis": draw_model_vis(jax.random.fold_in(seeds[6], 71), 0),
        "observed": centred(seeds[1], (CHANNELS, ROWS), 8.0, 48.0, ((0, 32),), jnp.float32),
        "row_keep": with_ends((jax.random.randint(seeds[2], (CHANNELS, ROWS), 0, 4) < 3).astype(jnp.int32), jax.random.fold_in(seeds[2], 1), 0, 1),
        "station_one": draw_station_one(jax.random.fold_in(seeds[6], 71), 0),
        "station_two": draw_station_two(jax.random.fold_in(seeds[6], 71), 0),
        "smoothness": jnp.clip(jnp.exp(jax.random.uniform(seeds[5], (BLOCK,), jnp.float32, math.log(4.0), math.log(24576.0))), 4.0, 24576.0),
    }


ridge_weight = 1.0

def product(left, right):
    return jnp.dot(left, right, precision=lax.Precision.HIGHEST)

def solve_with(factor, source):
    inner = jax.scipy.linalg.solve_triangular(factor, source, lower=True)
    return jax.scipy.linalg.solve_triangular(factor, inner, lower=True, trans=1)

def normal_system(model_channel, data_channel, keep_channel, station_one, station_two):
    coherence = model_channel.astype(jnp.float32).T
    weights = keep_channel.astype(jnp.float32)
    row_count = coherence.shape[0]
    outer_terms = (weights[:, None, None] * coherence[:, :, None] * coherence[:, None, :]).reshape(row_count, DIRECTIONS * DIRECTIONS)
    pair_one = station_one * STATIONS + station_two
    pair_two = station_two * STATIONS + station_one
    crossed = jax.ops.segment_sum(outer_terms, pair_one, STATIONS * STATIONS) + jax.ops.segment_sum(outer_terms, pair_two, STATIONS * STATIONS)
    selfed = jax.ops.segment_sum(outer_terms, station_one, STATIONS) + jax.ops.segment_sum(outer_terms, station_two, STATIONS)
    crossed = crossed.reshape(STATIONS, STATIONS, DIRECTIONS, DIRECTIONS)
    identity = jnp.eye(STATIONS, dtype=jnp.float32)
    blocks = crossed + identity[:, :, None, None] * selfed.reshape(STATIONS, 1, DIRECTIONS, DIRECTIONS)
    normal = blocks.transpose(2, 0, 3, 1).reshape(DIRECTIONS * STATIONS, DIRECTIONS * STATIONS)
    projected = (weights * data_channel)[:, None] * coherence
    target = jax.ops.segment_sum(projected, station_one, STATIONS) + jax.ops.segment_sum(projected, station_two, STATIONS)
    return (normal, target.T.reshape(DIRECTIONS * STATIONS))

def reference(model_vis, observed, row_keep, station_one, station_two, smoothness):
    block_width = smoothness.shape[0]
    identity = jnp.eye(block_width, dtype=jnp.float32)
    channels = jnp.arange(CHANNELS, dtype=jnp.int32)

    def forward(carried, channel_items):
        previous_inverse, previous_vector = carried
        model_channel, data_channel, keep_channel, channel = channel_items
        normal, target = normal_system(model_channel, data_channel, keep_channel, station_one, station_two)
        neighbours = 2.0 - (channel == 0).astype(jnp.float32) - (channel == CHANNELS - 1).astype(jnp.float32)
        pivot_block = normal + jnp.diag(ridge_weight + neighbours * smoothness) - smoothness[:, None] * previous_inverse * smoothness[None, :]
        source = target + smoothness * previous_vector
        factor = jnp.linalg.cholesky(pivot_block)
        inverse = solve_with(factor, identity)
        solved = product(inverse, source)
        return ((inverse, solved), (inverse * smoothness[None, :], solved))
    start = (jnp.zeros((block_width, block_width), jnp.float32), jnp.zeros((block_width,), jnp.float32))
    finished, stacked = lax.scan(forward, start, (model_vis, observed, row_keep, channels))

    def backward(later, channel_items):
        coupling, solved = channel_items
        current = solved + product(coupling, later)
        return (current, current)
    finished_back, gains = lax.scan(backward, jnp.zeros((block_width,), jnp.float32), stacked, reverse=True)
    return gains
```

```python
import jax
import jax.numpy as jnp
from jax import lax
from jax.experimental import pallas as pl
from jax.experimental.pallas import tpu as pltpu
from jax.sharding import PartitionSpec as P

ridge_weight = 1.0
PANEL = 128
GROUP = 16
HIGHEST = lax.Precision.HIGHEST


def mm(left, right, dims=((1,), (0,))):
    return lax.dot_general(
        left, right, (dims, ((), ())), precision=HIGHEST, preferred_element_type=jnp.float32
    )


NT = ((1,), (1,))
TN = ((0,), (0,))


def invert_panel(block):
    size = block.shape[0]
    lane = lax.broadcasted_iota(jnp.int32, (1, size), 1)
    sub = lax.broadcasted_iota(jnp.int32, (size, 1), 0)

    def group(_, a):
        for k in range(GROUP):
            row = a[k : k + 1, :]
            col = a[:, k : k + 1]
            inv = 1.0 / a[k : k + 1, k : k + 1]
            scaled = jnp.where(lane == k, 1.0, row) * inv
            factor = jnp.where(sub == k, -1.0, col)
            rest = jnp.where((lane == k) | (sub == k), 0.0, a)
            a = rest - factor * scaled
        a = jnp.concatenate([a[GROUP:, :], a[:GROUP, :]], axis=0)
        return pltpu.roll(a, size - GROUP, 1)

    return lax.fori_loop(0, size // GROUP, group, block)


def invert_in_place(a_ref, row_ref):
    width = a_ref.shape[0]

    @pl.loop(0, width // PANEL)
    def _(step):
        own = pl.ds(pl.multiple_of(step * PANEL, PANEL), PANEL)
        pivot = invert_panel(a_ref[own, own])
        row_ref[...] = mm(pivot, a_ref[own, :])
        row_ref[:, own] = pivot
        col = a_ref[:, own]
        a_ref[:, own] = jnp.zeros_like(col)
        a_ref[...] = a_ref[...] - mm(col, row_ref[...])
        a_ref[own, :] = row_ref[...]


def normal_kernel(vis_ref, obs_ref, keep_ref, one_ref, two_ref, normal_ref, target_ref):
    padded = normal_ref.shape[1]
    directions, rows = vis_ref.shape[1], vis_ref.shape[2]
    stations = padded // directions

    @pl.when(pl.program_id(1) == 0)
    def _():
        normal_ref[...] = jnp.zeros_like(normal_ref)
        target_ref[...] = jnp.zeros_like(target_ref)

    station = lax.broadcasted_iota(jnp.int32, (stations, rows), 0)
    touched = (station == one_ref[...]) | (station == two_ref[...])
    keep = keep_ref[0].astype(jnp.float32)
    vis = vis_ref[0].astype(jnp.float32)
    kept = touched & (keep > 0.0)
    plain = jnp.concatenate(
        [jnp.where(touched, vis[d : d + 1, :], 0.0) for d in range(directions)], axis=0
    ).astype(jnp.bfloat16)
    weighted = jnp.concatenate(
        [jnp.where(kept, vis[d : d + 1, :], 0.0) for d in range(directions)], axis=0
    ).astype(jnp.bfloat16)
    normal_ref[0] += lax.dot_general(
        weighted, plain, (NT, ((), ())), preferred_element_type=jnp.float32
    )
    data = obs_ref[0]
    high = data.astype(jnp.bfloat16).astype(jnp.float32)
    middle = (data - high).astype(jnp.bfloat16).astype(jnp.float32)
    low = data - high - middle
    pieces = jnp.concatenate([high, middle, low, jnp.zeros((5, rows), jnp.float32)], axis=0)
    target_ref[0] += lax.dot_general(
        pieces.astype(jnp.bfloat16), weighted, (NT, ((), ())), preferred_element_type=jnp.float32
    )


def first_kernel(diag_ref, source_ref, down_ref, across_ref, coupling_ref, y_ref, a_ref, row_ref):
    a_ref[...] = diag_ref[...]
    invert_in_place(a_ref, row_ref)
    y_ref[...] = mm(source_ref[...], a_ref[...])
    scaled = a_ref[...] * across_ref[...]
    coupling_ref[...] = scaled * down_ref[...]


def level_kernel(
    diag_ref, lower_ref, above_ref, source_ref,
    xr_ref, xl_ref, up_ref, down_ref, c_ref, y_ref, by_up_ref, by_down_ref, a_ref, row_ref,
):
    a_ref[...] = diag_ref[...]
    invert_in_place(a_ref, row_ref)
    xr_ref[...] = mm(above_ref[...], a_ref[...])
    xl_ref[...] = mm(lower_ref[...], a_ref[...], TN)
    up_ref[...] = mm(xr_ref[...], above_ref[...], NT)
    c_ref[...] = mm(xr_ref[...], lower_ref[...])
    down_ref[...] = mm(xl_ref[...], lower_ref[...])
    y = mm(source_ref[...], a_ref[...])
    y_ref[...] = y
    by_up_ref[...] = mm(y, above_ref[...], NT)
    by_down_ref[...] = mm(y, lower_ref[...])


def last_kernel(diag_ref, source_ref, y_ref, a_ref, row_ref):
    a_ref[...] = diag_ref[...]
    invert_in_place(a_ref, row_ref)
    y_ref[...] = mm(source_ref[...], a_ref[...])


def call(kernel, width, outs, *operands):
    vmem = pl.BlockSpec(memory_space=pltpu.VMEM)
    return pl.pallas_call(
        kernel,
        out_shape=[jax.ShapeDtypeStruct(o, jnp.float32) for o in outs],
        in_specs=[vmem] * len(operands),
        out_specs=[vmem] * len(outs),
        scratch_shapes=[
            pltpu.VMEM((width, width), jnp.float32),
            pltpu.VMEM((PANEL, width), jnp.float32),
        ],
        compiler_params=pltpu.CompilerParams(vmem_limit_bytes=48 << 20),
    )(*operands)


def normals(model_vis, observed, row_keep, station_one, station_two, padded):
    channels, directions, rows = model_vis.shape
    chunk = 1024 if rows % 1024 == 0 else rows
    return pl.pallas_call(
        normal_kernel,
        grid=(channels, rows // chunk),
        out_shape=[
            jax.ShapeDtypeStruct((channels, padded, padded), jnp.float32),
            jax.ShapeDtypeStruct((channels, 8, padded), jnp.float32),
        ],
        in_specs=[
            pl.BlockSpec((1, directions, chunk), lambda f, r: (f, 0, r)),
            pl.BlockSpec((1, 1, chunk), lambda f, r: (f, 0, r)),
            pl.BlockSpec((1, 1, chunk), lambda f, r: (f, 0, r)),
            pl.BlockSpec((1, chunk), lambda f, r: (0, r)),
            pl.BlockSpec((1, chunk), lambda f, r: (0, r)),
        ],
        out_specs=[
            pl.BlockSpec((1, padded, padded), lambda f, r: (f, 0, 0)),
            pl.BlockSpec((1, 8, padded), lambda f, r: (f, 0, 0)),
        ],
        compiler_params=pltpu.CompilerParams(vmem_limit_bytes=48 << 20),
    )(
        model_vis,
        observed.reshape(channels, 1, rows),
        row_keep.reshape(channels, 1, rows),
        station_one.reshape(1, rows),
        station_two.reshape(1, rows),
    )


def move(block, route):
    return lax.ppermute(block, "freq", route)


def body(model_vis, observed, row_keep, station_one, station_two, smoothness):
    channels, directions, _ = model_vis.shape
    assert channels == 2
    devices = lax.axis_size("freq")
    assert devices & (devices - 1) == 0
    position = lax.axis_index("freq")
    stations = smoothness.shape[0] // directions
    slots = -(-stations // 64) * 64
    width = directions * slots
    square, line = (width, width), (8, width)
    smooth = jnp.pad(
        smoothness.reshape(directions, stations), ((0, 0), (0, slots - stations))
    ).reshape(width)

    normal, pieces = normals(model_vis, observed, row_keep, station_one, station_two, width)
    targets = jnp.sum(pieces, axis=1)
    identity = jnp.eye(width, dtype=jnp.float32)

    def diagonal(local):
        channel = position * channels + local
        neighbours = (
            2.0
            - (channel == 0).astype(jnp.float32)
            - (channel == channels * devices - 1).astype(jnp.float32)
        )
        return normal[local] + identity * (ridge_weight + neighbours * smooth)[:, None]

    def as_line(vector):
        return jnp.pad(vector[None, :], ((0, 7), (0, 0)))

    coupling, y0 = call(
        first_kernel, width, (square, line),
        diagonal(0), as_line(targets[0]), smooth[:, None], smooth[None, :],
    )
    back = [(i, i - 1) for i in range(1, devices)]
    from_next = move(coupling, back)
    pulled = y0 * smooth[None, :]
    pulled_next = move(pulled, back)
    diag = diagonal(1) - coupling - from_next
    lower = -jnp.where(position > 0, coupling, 0.0)
    above = -from_next
    source = as_line(targets[1]) + pulled + pulled_next

    levels = (devices - 1).bit_length()
    kept = []
    for level in range(levels):
        stride = 1 << level
        xr, xl, up, down, cross, y, by_up, by_down = call(
            level_kernel, width, (square,) * 5 + (line,) * 3, diag, lower, above, source
        )
        kept.append((xr, xl, y))
        gone = range(stride - 1, devices, 2 * stride)
        rise = [(i, i + stride) for i in gone]
        fall = [(i, i - stride) for i in gone if i >= stride]
        next_gone = range(2 * stride - 1, devices, 4 * stride) if level + 1 < levels else ()
        if fall:
            diag = diag - move(up, rise) - move(down, fall)
            source = source - move(by_up, rise) - move(by_down, fall)
        else:
            diag = diag - move(up, rise)
            source = source - move(by_up, rise)
        if level + 1 < levels:
            lower = -move(cross, [(i, j) for i, j in rise if j in next_gone])
            above = -move(cross, [(i, j) for i, j in fall if j in next_gone])
    (gains,) = call(last_kernel, width, (line,), diag, source)
    for level in reversed(range(levels)):
        stride = 1 << level
        xr, xl, y = kept[level]
        gone = range(stride - 1, devices, 2 * stride)
        from_above = move(gains, [(i + stride, i) for i in gone])
        value = y - mm(from_above, xr)
        falling = [(i - stride, i) for i in gone if i >= stride]
        if falling:
            value = value - mm(move(gains, falling), xl)
        mine = lax.rem(position + 1, 2 * stride) == stride
        gains = jnp.where(mine, value, gains)
    earlier = move(gains, [(i, i + 1) for i in range(devices - 1)])
    scale = jnp.where(smooth > 0, 1.0 / jnp.where(smooth > 0, smooth, 1.0), 0.0)
    first = y0 + mm(earlier + gains, coupling) * scale[None, :]
    both = jnp.stack([first[0], gains[0]])
    return both.reshape(channels, directions, slots)[:, :, :stations].reshape(
        channels, directions * stations
    )


def solution(mesh):
    placed = (P("freq", None, None), P("freq", None), P("freq", None), P(), P(), P())
    return jax.shard_map(
        body, mesh=mesh, in_specs=placed, out_specs=P("freq", None), check_vma=False
    )
```

```python
import jax
import jax.numpy as jnp
from jax import lax
from jax.experimental import pallas as pl
from jax.experimental.pallas import tpu as pltpu
from jax.sharding import PartitionSpec as P

ridge_weight = 1.0
PANEL = 128
GROUP = 16
SUB = 8
PIVOTS = 4
HIGHEST = lax.Precision.HIGHEST


def mm(left, right, dims=((1,), (0,))):
    return lax.dot_general(
        left, right, (dims, ((), ())), precision=HIGHEST, preferred_element_type=jnp.float32
    )


NT = ((1,), (1,))
TN = ((0,), (0,))


def small_inverse(entries):
    size = len(entries)
    for m in range(size):
        inv = 1.0 / entries[m][m]
        scaled = [inv if j == m else entries[m][j] * inv for j in range(size)]
        entries = [
            scaled
            if i == m
            else [
                -(entries[i][m] * inv) if j == m else entries[i][j] - entries[i][m] * scaled[j]
                for j in range(size)
            ]
            for i in range(size)
        ]
    return entries


def invert_panel(block):
    size = block.shape[0]
    strips = size // SUB
    lane = lax.broadcasted_iota(jnp.int32, (SUB, size), 1)
    sub = lax.broadcasted_iota(jnp.int32, (SUB, size), 0)

    def spread(value):
        return jnp.broadcast_to(value, (SUB, size))

    def group(_, a):
        a = list(a)
        for k in range(0, GROUP, PIVOTS):
            home, offset = k // SUB, k % SUB
            rows = [spread(a[home][offset + i : offset + i + 1, :]) for i in range(PIVOTS)]
            entries = [
                [spread(row[:, k + j : k + j + 1]) for j in range(PIVOTS)] for row in rows
            ]
            inverse = small_inverse(entries)
            inside = (lane >= k) & (lane < k + PIVOTS)
            marked = [
                jnp.where(inside, jnp.where(lane == k + i, 1.0, 0.0), rows[i])
                for i in range(PIVOTS)
            ]
            scaled = [
                sum(inverse[i][j] * marked[j] for j in range(PIVOTS)) for i in range(PIVOTS)
            ]
            for t in range(strips):
                value = jnp.where(inside, 0.0, a[t])
                for i in range(PIVOTS):
                    value = value - spread(a[t][:, k + i : k + i + 1]) * scaled[i]
                if t == home:
                    for i in range(PIVOTS):
                        value = jnp.where(sub == offset + i, scaled[i], value)
                a[t] = value
        shift = GROUP // SUB
        return tuple(pltpu.roll(a[(t + shift) % strips], size - GROUP, 1) for t in range(strips))

    start = tuple(block[t * SUB : (t + 1) * SUB, :] for t in range(strips))
    return jnp.concatenate(lax.fori_loop(0, size // GROUP, group, start), axis=0)


def invert_in_place(a_ref, row_ref):
    width = a_ref.shape[0]

    @pl.loop(0, width // PANEL)
    def _(step):
        own = pl.ds(pl.multiple_of(step * PANEL, PANEL), PANEL)
        pivot = invert_panel(a_ref[own, own])
        row_ref[...] = mm(pivot, a_ref[own, :])
        row_ref[:, own] = pivot
        col = a_ref[:, own]
        a_ref[:, own] = jnp.zeros_like(col)
        a_ref[...] = a_ref[...] - mm(col, row_ref[...])
        a_ref[own, :] = row_ref[...]


def normal_kernel(vis_ref, obs_ref, keep_ref, one_ref, two_ref, normal_ref, target_ref):
    padded = normal_ref.shape[1]
    directions, rows = vis_ref.shape[1], vis_ref.shape[2]
    stations = padded // directions

    @pl.when(pl.program_id(1) == 0)
    def _():
        normal_ref[...] = jnp.zeros_like(normal_ref)
        target_ref[...] = jnp.zeros_like(target_ref)

    station = lax.broadcasted_iota(jnp.int32, (stations, rows), 0)
    touched = (station == one_ref[...]) | (station == two_ref[...])
    keep = keep_ref[0].astype(jnp.float32)
    vis = vis_ref[0].astype(jnp.float32)
    kept = touched & (keep > 0.0)
    plain = jnp.concatenate(
        [jnp.where(touched, vis[d : d + 1, :], 0.0) for d in range(directions)], axis=0
    ).astype(jnp.bfloat16)
    weighted = jnp.concatenate(
        [jnp.where(kept, vis[d : d + 1, :], 0.0) for d in range(directions)], axis=0
    ).astype(jnp.bfloat16)
    normal_ref[0] += lax.dot_general(
        weighted, plain, (NT, ((), ())), preferred_element_type=jnp.float32
    )
    data = obs_ref[0]
    high = data.astype(jnp.bfloat16).astype(jnp.float32)
    middle = (data - high).astype(jnp.bfloat16).astype(jnp.float32)
    low = data - high - middle
    pieces = jnp.concatenate([high, middle, low, jnp.zeros((5, rows), jnp.float32)], axis=0)
    target_ref[0] += lax.dot_general(
        pieces.astype(jnp.bfloat16), weighted, (NT, ((), ())), preferred_element_type=jnp.float32
    )


def first_kernel(diag_ref, source_ref, down_ref, across_ref, coupling_ref, y_ref, a_ref, row_ref):
    a_ref[...] = diag_ref[...]
    invert_in_place(a_ref, row_ref)
    y_ref[...] = mm(source_ref[...], a_ref[...])
    scaled = a_ref[...] * across_ref[...]
    coupling_ref[...] = scaled * down_ref[...]


def level_kernel(
    diag_ref, lower_ref, above_ref, source_ref,
    xr_ref, xl_ref, up_ref, down_ref, c_ref, y_ref, by_up_ref, by_down_ref, a_ref, row_ref,
):
    a_ref[...] = diag_ref[...]
    invert_in_place(a_ref, row_ref)
    xr_ref[...] = mm(above_ref[...], a_ref[...])
    xl_ref[...] = mm(lower_ref[...], a_ref[...], TN)
    up_ref[...] = mm(xr_ref[...], above_ref[...], NT)
    c_ref[...] = mm(xr_ref[...], lower_ref[...])
    down_ref[...] = mm(xl_ref[...], lower_ref[...])
    y = mm(source_ref[...], a_ref[...])
    y_ref[...] = y
    by_up_ref[...] = mm(y, above_ref[...], NT)
    by_down_ref[...] = mm(y, lower_ref[...])


def last_kernel(diag_ref, source_ref, y_ref, a_ref, row_ref):
    a_ref[...] = diag_ref[...]
    invert_in_place(a_ref, row_ref)
    y_ref[...] = mm(source_ref[...], a_ref[...])


def call(kernel, width, outs, *operands):
    vmem = pl.BlockSpec(memory_space=pltpu.VMEM)
    return pl.pallas_call(
        kernel,
        out_shape=[jax.ShapeDtypeStruct(o, jnp.float32) for o in outs],
        in_specs=[vmem] * len(operands),
        out_specs=[vmem] * len(outs),
        scratch_shapes=[
            pltpu.VMEM((width, width), jnp.float32),
            pltpu.VMEM((PANEL, width), jnp.float32),
        ],
        compiler_params=pltpu.CompilerParams(vmem_limit_bytes=48 << 20),
    )(*operands)


def normals(model_vis, observed, row_keep, station_one, station_two, padded):
    channels, directions, rows = model_vis.shape
    chunk = 1024 if rows % 1024 == 0 else rows
    return pl.pallas_call(
        normal_kernel,
        grid=(channels, rows // chunk),
        out_shape=[
            jax.ShapeDtypeStruct((channels, padded, padded), jnp.float32),
            jax.ShapeDtypeStruct((channels, 8, padded), jnp.float32),
        ],
        in_specs=[
            pl.BlockSpec((1, directions, chunk), lambda f, r: (f, 0, r)),
            pl.BlockSpec((1, 1, chunk), lambda f, r: (f, 0, r)),
            pl.BlockSpec((1, 1, chunk), lambda f, r: (f, 0, r)),
            pl.BlockSpec((1, chunk), lambda f, r: (0, r)),
            pl.BlockSpec((1, chunk), lambda f, r: (0, r)),
        ],
        out_specs=[
            pl.BlockSpec((1, padded, padded), lambda f, r: (f, 0, 0)),
            pl.BlockSpec((1, 8, padded), lambda f, r: (f, 0, 0)),
        ],
        compiler_params=pltpu.CompilerParams(vmem_limit_bytes=48 << 20),
    )(
        model_vis,
        observed.reshape(channels, 1, rows),
        row_keep.reshape(channels, 1, rows),
        station_one.reshape(1, rows),
        station_two.reshape(1, rows),
    )


def move(block, route):
    return lax.ppermute(block, "freq", route)


def body(model_vis, observed, row_keep, station_one, station_two, smoothness):
    channels, directions, _ = model_vis.shape
    assert channels == 2
    devices = lax.axis_size("freq")
    assert devices & (devices - 1) == 0
    position = lax.axis_index("freq")
    stations = smoothness.shape[0] // directions
    slots = -(-stations // 64) * 64
    width = directions * slots
    square, line = (width, width), (8, width)
    smooth = jnp.pad(
        smoothness.reshape(directions, stations), ((0, 0), (0, slots - stations))
    ).reshape(width)

    normal, pieces = normals(model_vis, observed, row_keep, station_one, station_two, width)
    targets = jnp.sum(pieces, axis=1)
    identity = jnp.eye(width, dtype=jnp.float32)

    def diagonal(local):
        channel = position * channels + local
        neighbours = (
            2.0
            - (channel == 0).astype(jnp.float32)
            - (channel == channels * devices - 1).astype(jnp.float32)
        )
        return normal[local] + identity * (ridge_weight + neighbours * smooth)[:, None]

    def as_line(vector):
        return jnp.pad(vector[None, :], ((0, 7), (0, 0)))

    coupling, y0 = call(
        first_kernel, width, (square, line),
        diagonal(0), as_line(targets[0]), smooth[:, None], smooth[None, :],
    )
    back = [(i, i - 1) for i in range(1, devices)]
    from_next = move(coupling, back)
    pulled = y0 * smooth[None, :]
    pulled_next = move(pulled, back)
    diag = diagonal(1) - coupling - from_next
    lower = -jnp.where(position > 0, coupling, 0.0)
    above = -from_next
    source = as_line(targets[1]) + pulled + pulled_next

    levels = (devices - 1).bit_length()
    kept = []
    for level in range(levels):
        stride = 1 << level
        xr, xl, up, down, cross, y, by_up, by_down = call(
            level_kernel, width, (square,) * 5 + (line,) * 3, diag, lower, above, source
        )
        kept.append((xr, xl, y))
        gone = range(stride - 1, devices, 2 * stride)
        rise = [(i, i + stride) for i in gone]
        fall = [(i, i - stride) for i in gone if i >= stride]
        next_gone = range(2 * stride - 1, devices, 4 * stride) if level + 1 < levels else ()
        if fall:
            diag = diag - move(up, rise) - move(down, fall)
            source = source - move(by_up, rise) - move(by_down, fall)
        else:
            diag = diag - move(up, rise)
            source = source - move(by_up, rise)
        if level + 1 < levels:
            lower = -move(cross, [(i, j) for i, j in rise if j in next_gone])
            above = -move(cross, [(i, j) for i, j in fall if j in next_gone])
    (gains,) = call(last_kernel, width, (line,), diag, source)
    for level in reversed(range(levels)):
        stride = 1 << level
        xr, xl, y = kept[level]
        gone = range(stride - 1, devices, 2 * stride)
        from_above = move(gains, [(i + stride, i) for i in gone])
        value = y - mm(from_above, xr)
        falling = [(i - stride, i) for i in gone if i >= stride]
        if falling:
            value = value - mm(move(gains, falling), xl)
        mine = lax.rem(position + 1, 2 * stride) == stride
        gains = jnp.where(mine, value, gains)
    earlier = move(gains, [(i, i + 1) for i in range(devices - 1)])
    scale = jnp.where(smooth > 0, 1.0 / jnp.where(smooth > 0, smooth, 1.0), 0.0)
    first = y0 + mm(earlier + gains, coupling) * scale[None, :]
    both = jnp.stack([first[0], gains[0]])
    return both.reshape(channels, directions, slots)[:, :, :stations].reshape(
        channels, directions * stations
    )


def solution(mesh):
    placed = (P("freq", None, None), P("freq", None), P("freq", None), P(), P(), P())
    return jax.shard_map(
        body, mesh=mesh, in_specs=placed, out_specs=P("freq", None), check_vma=False
    )
```
